768 devices in a mesh: energy: 2 (over core), mom: 96 (over z, y), slab: 4 (over x).
Axes of the slice: x: 4, y: 8, z: 12, core: 2. Of those that a mesh axis runs over, the one named last changes fastest.
Arguments:
- green_blocks: float32 [4, 8, 768, 64, 128], P(None, 'slab', ('energy', 'mom')), may hold values from -1 to 1
- coupling: float32 [4, 4, 4], replicated, may hold values from 0.05 to 0.5
- deformation: float32 [4, 8, 64, 64], P(None, 'slab'), may hold values from -0.75 to 0.75
- phonon_shifts: int32 [4], replicated, may hold values from -2 to 2, as said below
Outputs:
- green_born: float32 [4, 8, 768, 64, 128], P(None, 'slab', ('energy', 'mom'))
- self_energy: float32 [4, 8, 768, 64, 128], P(None, 'slab', ('energy', 'mom'))
The draws below stay inside these ranges and needn't reach their ends.
Inputs may be any that keep to these rules, and one draw needn't show every extreme that they name: `phonon_shifts`: branches come in pairs 2j, 2j+1 with opposite offsets; branches 0 and 1 have offsets 2 and -2, the others a magnitude of 1 to 2.
All inputs are finite; a program needn't handle non-finite values.
Results may differ from the reference program's by a relative error of at most 0.0001.
Values sent between devices are 32-bit elements; how exact they have to be, the bound alone decides.
No kernel may reach another device: no remote copies, remote signals or barrier semaphores. Data moves between devices by JAX's collectives and lax.ppermute only.
A program may use at most 32 MiB of HBM per device.

```python
import math
import jax
import jax.numpy as jnp
from jax import lax

B = 64
NK = 4
NMODE = 4
W = 2
NE = 768
NS = 8


def draw_phonon_shifts(key, part):
    second = jax.random.randint(jax.random.fold_in(key, 7), (), 1, W + 1).astype(jnp.int32)
    largest = jnp.int32(W)
    return jnp.stack([largest, -largest, second, -second]).astype(jnp.int32)


def steps_of(stream_key, shape, split, smallest, high):
    def one(position, blocks):
        heights = jax.random.uniform(jax.random.fold_in(jax.random.fold_in(stream_key, 6), position), (blocks,), jnp.float32, smallest / len(split), high / len(split))
        return jnp.repeat(jnp.exp(heights), shape[position] // blocks).reshape((-1,) + (1,) * (len(shape) - position - 1))

    loudness = one(*split[0])
    for cut in split[1:]:
        loudness = loudness * one(*cut)
    return loudness


def gaussian(own_key, dims, deviation, bound, split=(), dtype=jnp.bfloat16):
    drawn = jax.random.normal(own_key, dims, jnp.float32) * deviation
    if len(split) > 0:
        drawn = steps_of(own_key, dims, split, -0.22, 0.18) * drawn
    return jnp.clip(drawn, min=-bound, max=bound).astype(dtype)


def setup_inputs(seed: int = 0) -> dict:
    key_list = jax.random.split(jax.random.key(seed), 5)
    return {
        "green_blocks": gaussian(key_list[0], (NK, NS, NE, B, 2 * B), 0.125, 1.0, ((1, 4), (2, 192)), jnp.float32),
        "coupling": jnp.clip(jnp.exp(jax.random.uniform(key_list[1], (NMODE, NK, NK), jnp.float32, math.log(0.05), math.log(0.5))), 0.05, 0.5),
        "deformation": gaussian(key_list[2], (NMODE, NS, B, B), B ** -0.5, 0.75, ((1, 4),), jnp.float32),
        "phonon_shifts": draw_phonon_shifts(jax.random.fold_in(key_list[4], 71), 0),
    }


neighbour_weight = 0.5


def complex_matrix(block):
    half = block.shape[-1] // 2
    real_part = block[..., :half]
    imag_part = block[..., half:]
    upper = jnp.concatenate([real_part, imag_part], axis=-1)
    lower = jnp.concatenate([-imag_part, real_part], axis=-1)
    return jnp.concatenate([upper, lower], axis=-2)


def complex_product(left, right):
    return jnp.einsum('...ij,...jk->...ik', left, complex_matrix(right), precision=lax.Precision.HIGHEST)


def block_transpose(deform):
    flipped = jnp.swapaxes(deform, -1, -2)
    blank = jnp.zeros_like(flipped)
    upper = jnp.concatenate([flipped, blank], axis=-1)
    lower = jnp.concatenate([blank, flipped], axis=-1)
    return jnp.concatenate([upper, lower], axis=-2)


def branch_term(field, mix_row, deform):
    mixed = jnp.einsum('kn,nsebc->ksebc', mix_row, field, precision=lax.Precision.HIGHEST)
    left = jnp.einsum('sij,ksejc->kseic', deform, mixed, precision=lax.Precision.HIGHEST)
    return jnp.einsum('kseic,scd->kseid', left, block_transpose(deform), precision=lax.Precision.HIGHEST)


def scatter_energy(green, coupling, deformation, phonon_shifts):
    summed = jnp.zeros(green.shape, jnp.float32)
    for branch in range(NMODE):
        term = branch_term(green, coupling[branch], deformation[branch])
        padded = jnp.pad(term, ((0, 0), (0, 0), (W, W), (0, 0), (0, 0)))
        offset = (W + phonon_shifts[branch]).astype(jnp.int32)
        summed = summed + lax.dynamic_slice_in_dim(padded, offset, NE, axis=2)
    rimmed = jnp.pad(summed, ((0, 0), (1, 1), (0, 0), (0, 0), (0, 0)))
    return summed + neighbour_weight * (rimmed[:, :-2] + rimmed[:, 2:])


def reference(green_blocks, coupling, deformation, phonon_shifts):
    first = scatter_energy(green_blocks, coupling, deformation, phonon_shifts)
    green_born = green_blocks + complex_product(complex_product(green_blocks, first), green_blocks)
    self_energy = scatter_energy(green_born, coupling, deformation, phonon_shifts)
    return green_born, self_energy
```

```python
import functools

import jax
import jax.numpy as jnp
from jax import lax
from jax.experimental import pallas as pl
from jax.experimental.pallas import tpu as pltpu
from jax.sharding import PartitionSpec as P

W = 2
neighbour_weight = 0.5

VMEM = pl.BlockSpec(memory_space=pltpu.VMEM)
ANY = pl.BlockSpec(memory_space=pl.ANY)
SMEM = pl.BlockSpec(memory_space=pltpu.SMEM)


PARAMS = pltpu.CompilerParams(vmem_limit_bytes=24 * 2**20)


def near(*arrays):
    return [pltpu.with_memory_space_constraint(x, pltpu.VMEM) for x in arrays]


def split(x):
    high = x.astype(jnp.bfloat16)
    low = (x - high.astype(jnp.float32)).astype(jnp.bfloat16)
    return high, low


def dot(a, b):
    return jnp.dot(a, b, preferred_element_type=jnp.float32)


def keep(high_all, low_all, s, place, blocks):
    high, low = split(jnp.concatenate(blocks, axis=0))
    high_all[s, place] = high
    low_all[s, place] = low


def prepare_kernel(coupling, deform, green, mixer, closer, high_all, low_all):
    modes, slabs, size, _ = deform.shape
    momenta = coupling.shape[1]
    for s in range(slabs):
        for e in range(green.shape[2]):
            keep(high_all, low_all, s, W + e, [green[k, s, e] for k in range(momenta)])
        for m in range(modes):
            d = deform[m, s]
            wide = jnp.concatenate([d] * momenta, axis=1)
            column = lax.broadcasted_iota(jnp.int32, wide.shape, 1) // size
            rows = []
            for k in range(momenta):
                weight = jnp.full(wide.shape, coupling[m, k, 0], jnp.float32)
                for k2 in range(1, momenta):
                    weight = jnp.where(column == k2, coupling[m, k, k2], weight)
                rows.append(weight * wide)
            high, low = split(jnp.concatenate(rows, axis=0))
            mixer[m, s] = jnp.concatenate([high, low], axis=1)
            flipped = d.T
            blank = jnp.zeros_like(flipped)
            both = jnp.concatenate(
                [
                    jnp.concatenate([flipped, blank], axis=1),
                    jnp.concatenate([blank, flipped], axis=1),
                ],
                axis=0,
            )
            high, low = split(both)
            closer[s, pl.ds(m * 2 * size, 2 * size), :] = jnp.concatenate([high, low], axis=1)


def halves(momenta, slabs, energies, size, width):
    return [pltpu.VMEM((slabs, energies + 2 * W, momenta * size, width), jnp.bfloat16)] * 2


def prepare(coupling, deformation, green):
    modes, slabs, size, _ = deformation.shape
    kron = coupling.shape[1] * size
    return pl.pallas_call(
        prepare_kernel,
        out_shape=(
            pltpu.VMEM((modes, slabs, kron, 2 * kron), jnp.bfloat16),
            pltpu.VMEM((slabs, modes * 2 * size, 4 * size), jnp.bfloat16),
            *halves(*green.shape),
        ),
        in_specs=[SMEM, VMEM, VMEM],
        out_specs=(VMEM,) * 4,
        compiler_params=PARAMS,
        name="prepare",
    )(coupling, *near(deformation, green))


def scatter_kernel(edges, targets, info, mixer, closer, high_all, low_all, *refs):
    if edges:
        first, second = refs[:2]
        high_all, low_all = refs[-2:]
    out, to_first, to_second = refs[2:5] if edges else refs
    slabs, _, kron, width = high_all.shape
    momenta, _, _, size, _ = out.shape
    modes = mixer.shape[0]
    odd_energy, odd_slab = info[modes], info[modes + 1]
    if edges:
        before, after = edges
        for s in range(slabs):
            for i in range(first.shape[2]):
                for piece, odd, even in ((first, before, after), (second, after, before)):
                    place = jnp.where(odd_energy == 1, odd + i, even + i)
                    keep(high_all, low_all, s, place, [piece[k, s, i] for k in range(momenta)])
    for s in range(slabs):
        for p in range(0, len(targets), 2):
            pair = targets[p : p + 2]
            highs, lows = [], []
            for m in range(modes):
                at = [e + W + info[m] for e in pair]
                gh = jnp.concatenate([high_all[s, a] for a in at], axis=1)
                gl = jnp.concatenate([low_all[s, a] for a in at], axis=1)
                mh = mixer[m, s, :, :kron]
                ml = mixer[m, s, :, kron:]
                left = dot(
                    jnp.concatenate([mh, mh, ml], axis=1),
                    jnp.concatenate([gh, gl, gh], axis=0),
                )
                high, low = split(left)
                highs.append(jnp.concatenate([high[:, :width], high[:, width:]], axis=0))
                lows.append(jnp.concatenate([low[:, :width], low[:, width:]], axis=0))
            high = jnp.concatenate(highs, axis=1)
            low = jnp.concatenate(lows, axis=1)
            both = dot(high, closer[s])
            rest = dot(low, closer[s, :, :width])
            total = both[:, :width] + both[:, width:] + rest
            for i in range(2):
                for k in range(momenta):
                    row = i * kron + k * size
                    out[k, s, p + i] = total[row : row + size]
    top = jnp.where(odd_slab == 1, 0, slabs - 1)
    for k in range(momenta):
        to_first[k, 0] = out[k, top]
        to_second[k, 0] = out[k, slabs - 1 - top]


def scatter(info, mixer, closer, field, targets, momenta, halo=(), edges=()):
    slabs, _, kron, width = field[0].shape
    size = kron // momenta
    edge = pltpu.VMEM((momenta, 1, len(targets), size, width), jnp.float32)
    kept = [pltpu.VMEM(x.shape, x.dtype) for x in field] if edges else []
    *made, = pl.pallas_call(
        functools.partial(scatter_kernel, edges, targets),
        out_shape=(
            pltpu.VMEM((momenta, slabs, len(targets), size, width), jnp.float32),
            edge,
            edge,
            *kept,
        ),
        in_specs=[SMEM] + [VMEM] * (4 + len(halo)),
        out_specs=(VMEM,) * (3 + len(kept)),
        input_output_aliases={3: 3, 4: 4} if edges else {},
        compiler_params=PARAMS,
        name="scatter",
    )(info, *near(mixer, closer, *field, *halo))
    return made[0], made[1], made[2], made[3:] or field


def complex_matrix(block, sign):
    half = block.shape[-1] // 2
    swapped = jnp.concatenate([block[:, half:], block[:, :half]], axis=1)
    return jnp.concatenate([block, swapped * sign], axis=0)


def complex_product(left, right, sign):
    rows, width = left.shape
    lh, ll = split(left)
    rh, rl = split(complex_matrix(right, sign))
    y = dot(jnp.concatenate([lh, ll], axis=0), jnp.concatenate([rh, rl], axis=1))
    return y[:rows, :width] + y[:rows, width:] + y[rows:, :width]


def rim(summed, k, s, first, second, odd):
    slabs = summed.shape[1]
    lower = summed[k, s - 1] if s > 0 else jnp.where(odd == 1, first[k, 0], second[k, 0])
    upper = summed[k, s + 1] if s + 1 < slabs else jnp.where(odd == 1, second[k, 0], first[k, 0])
    return summed[k, s] + neighbour_weight * (lower + upper)


def born_kernel(targets, earlier, info, green, summed, first, second, *refs):
    done = refs[0] if earlier else None
    out, to_first, to_second, high_all, low_all = refs[-5:]
    momenta, slabs, _, size, width = green.shape
    odd_energy, odd_slab = info[info.shape[0] - 2], info[info.shape[0] - 1]
    lane = lax.broadcasted_iota(jnp.int32, (size, width), 1)
    sign = jnp.where(lane < width // 2, -1.0, 1.0).astype(jnp.float32)
    place = {e: e for e in targets} if earlier else {e: i for i, e in enumerate(targets)}
    for s in range(slabs):
        for k in range(momenta):
            field = rim(summed, k, s, first, second, odd_slab)
            made = []
            for i, e in enumerate(targets):
                g = green[k, s, e]
                new = g + complex_product(complex_product(g, field[i], sign), g, sign)
                out[k, s, place[e]] = new
                high, low = split(new)
                high_all[s, W + e, k * size : (k + 1) * size] = high
                low_all[s, W + e, k * size : (k + 1) * size] = low
                made.append(new)
            to_first[k, s, 0] = jnp.where(odd_energy == 1, made[0], made[1])
            to_second[k, s, 0] = jnp.where(odd_energy == 1, made[1], made[0])
            for i, e in enumerate(earlier):
                out[k, s, e] = done[k, s, i]


def born(info, green, summed, first, second, targets, earlier=(), done=(), field=()):
    momenta, slabs, energies, size, width = green.shape
    held = energies if earlier else len(targets)
    halo = pltpu.VMEM((momenta, slabs, 1, size, width), jnp.float32)
    *made, = pl.pallas_call(
        functools.partial(born_kernel, targets, earlier),
        out_shape=(
            pltpu.VMEM((momenta, slabs, held, size, width), jnp.float32),
            halo,
            halo,
            *halves(*green.shape),
        ),
        in_specs=[SMEM] + [VMEM] * (4 + len(done) + len(field)),
        out_specs=(VMEM,) * 5,
        input_output_aliases={6: 3, 7: 4} if field else {},
        compiler_params=PARAMS,
        name="born",
    )(info, *near(green, summed, first, second, *done, *field))
    return made[0], made[1], made[2], made[3:]


def join_kernel(targets, info, summed, first, second, *refs):
    out, held, sems = refs[-3:]
    momenta, slabs = summed.shape[:2]
    odd_slab = info[info.shape[0] - 1]
    for k in range(momenta):
        for s in range(slabs):
            held[k, s] = rim(summed, k, s, first, second, odd_slab)
    copies = [
        pltpu.make_async_copy(
            held.at[:, :, pl.ds(i, 1)], out.at[:, :, pl.ds(e, 1)], sems.at[i]
        )
        for i, e in enumerate(targets)
    ]
    for copy in copies:
        copy.start()
    for copy in copies:
        copy.wait()


def join(info, summed, first, second, targets, energies, earlier=()):
    momenta, slabs, _, size, width = summed.shape
    return pl.pallas_call(
        functools.partial(join_kernel, targets),
        out_shape=jax.ShapeDtypeStruct((momenta, slabs, energies, size, width), jnp.float32),
        in_specs=[SMEM] + [VMEM] * 3 + [ANY] * len(earlier),
        out_specs=ANY,
        scratch_shapes=[
            pltpu.VMEM(summed.shape, jnp.float32),
            pltpu.SemaphoreType.DMA((len(targets),)),
        ],
        input_output_aliases={4: 0} if earlier else {},
        compiler_params=PARAMS,
        name="join",
    )(info, *near(summed, first, second), *earlier)


ENERGY = ("energy", "mom")


def pairs(size, start):
    return [p for i in range(start, size - 1, 2) for p in ((i, i + 1), (i + 1, i))]


def swap_energy(to_first, to_second):
    size = lax.axis_size(ENERGY)
    return [lax.ppermute(x, ENERGY, pairs(size, i)) for i, x in enumerate((to_first, to_second))]


def swap_slab(to_first, to_second):
    cores, size = lax.axis_size("energy"), lax.axis_size("slab")
    received = []
    for i, x in enumerate((to_first, to_second)):
        both = [
            (c * size + a, c * size + b)
            for c in range(cores)
            for a, b in pairs(size, (i + c) % 2)
        ]
        received.append(lax.ppermute(x, ("energy", "slab"), both))
    return received


def on_device(green, coupling, deformation, phonon_shifts):
    momenta, slabs, energies = green.shape[:3]
    odd_energy = lax.axis_index(ENERGY) & 1
    odd_slab = (lax.axis_index("slab") + lax.axis_index("energy")) & 1
    info = jnp.concatenate([phonon_shifts, odd_energy[None], odd_slab[None]]).astype(jnp.int32)
    inner = tuple(range(1, energies - 1))
    outer = (0, energies - 1)
    far = energies - W

    to_first = lax.dynamic_slice_in_dim(green, jnp.where(odd_energy == 1, 0, far), W, axis=2)
    to_second = lax.dynamic_slice_in_dim(green, jnp.where(odd_energy == 1, far, 0), W, axis=2)
    halo = swap_energy(to_first, to_second)
    mixer, closer, *field = prepare(coupling, deformation, green)

    def sums(field, targets, halo=(), edges=()):
        summed, a, b, field = scatter(info, mixer, closer, field, targets, momenta, halo, edges)
        return summed, swap_slab(a, b), field

    outer_sum, outer_rim, field = sums(field, outer, halo, (0, W + energies))
    inner_sum, inner_rim, _ = sums(field, inner)

    outer_born, a, b, field = born(info, green, outer_sum, *outer_rim, outer)
    near_halo = swap_energy(a, b)
    green_born, a, b, field = born(
        info, green, inner_sum, *inner_rim, inner, outer, (outer_born,), field
    )
    far_halo = swap_energy(a, b)

    inner_sum, inner_rim, field = sums(field, inner, near_halo, (W - 1, W + energies))
    outer_sum, outer_rim, _ = sums(field, outer, far_halo, (0, W + energies + 1))
    half = join(info, inner_sum, *inner_rim, inner, energies)
    return green_born, join(info, outer_sum, *outer_rim, outer, energies, (half,))


def solution(mesh):
    spread = P(None, "slab", ENERGY, None, None)
    return jax.shard_map(
        on_device,
        mesh=mesh,
        in_specs=(spread, P(), P(None, "slab", None, None), P()),
        out_specs=(spread, spread),
        check_vma=False,
    )
```

```python
import functools

import jax
import jax.numpy as jnp
from jax import lax
from jax.experimental import pallas as pl
from jax.experimental.pallas import tpu as pltpu
from jax.sharding import PartitionSpec as P

W = 2
neighbour_weight = 0.5

VMEM = pl.BlockSpec(memory_space=pltpu.VMEM)
ANY = pl.BlockSpec(memory_space=pl.ANY)
SMEM = pl.BlockSpec(memory_space=pltpu.SMEM)


PARAMS = pltpu.CompilerParams(vmem_limit_bytes=24 * 2**20)


def near(*arrays):
    return [pltpu.with_memory_space_constraint(x, pltpu.VMEM) for x in arrays]


def split(x):
    high = x.astype(jnp.bfloat16)
    low = (x - high.astype(jnp.float32)).astype(jnp.bfloat16)
    return high, low


def dot(a, b):
    return jnp.dot(a, b, preferred_element_type=jnp.float32)


def keep(high_all, low_all, s, place, blocks):
    high, low = split(jnp.concatenate(blocks, axis=0))
    high_all[s, place] = high
    low_all[s, place] = low


def prepare_kernel(coupling, deform, green, mixer, closer, high_all, low_all):
    modes, slabs, size, _ = deform.shape
    momenta = coupling.shape[1]
    for s in range(slabs):
        for e in range(green.shape[2]):
            keep(high_all, low_all, s, e, [green[k, s, e] for k in range(momenta)])
        for m in range(modes):
            d = deform[m, s]
            wide = jnp.concatenate([d] * momenta, axis=1)
            column = lax.broadcasted_iota(jnp.int32, wide.shape, 1) // size
            rows = []
            for k in range(momenta):
                weight = jnp.full(wide.shape, coupling[m, k, 0], jnp.float32)
                for k2 in range(1, momenta):
                    weight = jnp.where(column == k2, coupling[m, k, k2], weight)
                rows.append(weight * wide)
            high, low = split(jnp.concatenate(rows, axis=0))
            mixer[m, s] = jnp.concatenate([high, low], axis=1)
            flipped = d.T
            blank = jnp.zeros_like(flipped)
            both = jnp.concatenate(
                [
                    jnp.concatenate([flipped, blank], axis=1),
                    jnp.concatenate([blank, flipped], axis=1),
                ],
                axis=0,
            )
            high, low = split(both)
            closer[s, pl.ds(m * 2 * size, 2 * size), :] = jnp.concatenate([high, low], axis=1)


def halves(momenta, slabs, energies, size, width):
    return [pltpu.VMEM((slabs, energies, momenta * size, width), jnp.bfloat16)] * 2


def prepare(coupling, deformation, green):
    modes, slabs, size, _ = deformation.shape
    kron = coupling.shape[1] * size
    return pl.pallas_call(
        prepare_kernel,
        out_shape=(
            pltpu.VMEM((modes, slabs, kron, 2 * kron), jnp.bfloat16),
            pltpu.VMEM((slabs, modes * 2 * size, 4 * size), jnp.bfloat16),
            *halves(*green.shape),
        ),
        in_specs=[SMEM, VMEM, VMEM],
        out_specs=(VMEM,) * 4,
        compiler_params=PARAMS,
        name="prepare",
    )(coupling, *near(deformation, green))


def turn_of(info, energies, turn):
    up = info[info.shape[0] - 2] ^ (1 - turn)
    return up, up * (energies // 2)


def branch_sums(info, mixer, closer, high_all, low_all, s, places, up):
    modes, _, kron, _ = mixer.shape
    width = high_all.shape[3]
    highs, lows, ends = [], [], []
    for j in range(0, modes, 2):
        m = j + jnp.where((info[j] > 0) == (up == 1), 0, 1)
        at = [p + info[m] for p in places]
        gh = jnp.concatenate([high_all[s, a] for a in at], axis=1)
        gl = jnp.concatenate([low_all[s, a] for a in at], axis=1)
        mh = mixer[m, s, :, :kron]
        ml = mixer[m, s, :, kron:]
        left = dot(
            jnp.concatenate([mh, mh, ml], axis=1),
            jnp.concatenate([gh, gl, gh], axis=0),
        )
        high, low = split(left)
        count = len(places)
        highs.append(
            jnp.concatenate([high[:, i * width : (i + 1) * width] for i in range(count)], axis=0)
        )
        lows.append(
            jnp.concatenate([low[:, i * width : (i + 1) * width] for i in range(count)], axis=0)
        )
        ends.append(closer[s, pl.ds(pl.multiple_of(m * width, width), width), :])
    end = jnp.concatenate(ends, axis=0)
    both = dot(jnp.concatenate(highs, axis=1), end)
    rest = dot(jnp.concatenate(lows, axis=1), end[:, :width])
    return both[:, :width] + both[:, width:] + rest


def own_kernel(info, mixer, closer, high_all, low_all, out):
    momenta, slabs, energies, size, _ = out.shape
    half = energies // 2
    for s in range(slabs):
        for up in (1, 0):
            targets = range((1 - up) * half, (2 - up) * half)
            total = branch_sums(info, mixer, closer, high_all, low_all, s, targets, up)
            for i, e in enumerate(targets):
                for k in range(momenta):
                    row = (i * momenta + k) * size
                    out[k, s, e] = total[row : row + size]


def own_part(info, mixer, closer, field, shape):
    return pl.pallas_call(
        own_kernel,
        out_shape=pltpu.VMEM(shape, jnp.float32),
        in_specs=[SMEM] + [VMEM] * 4,
        out_specs=VMEM,
        compiler_params=PARAMS,
        name="own_part",
    )(info, *near(mixer, closer, *field))


def halo_kernel(turn, info, mixer, closer, high_own, low_own, part, halo, *refs):
    out, to_first, to_second, high_run, low_run = refs
    momenta, slabs, energies, size, _ = part.shape
    half = energies // 2
    up, start = turn_of(info, energies, turn)
    for s in range(slabs):
        for i in range(W - 1):
            own = jnp.where(up == 1, energies - W + 1 + i, i)
            place = jnp.where(up == 1, i, W + i)
            high_run[s, place] = high_own[s, own]
            low_run[s, place] = low_own[s, own]
        for i in range(W):
            place = jnp.where(up == 1, W - 1 + i, i)
            keep(high_run, low_run, s, place, [halo[k, s, i] for k in range(momenta)])
        shift = jnp.where(up == 1, -1, W)
        places = [i + shift for i in range(half)]
        total = branch_sums(info, mixer, closer, high_run, low_run, s, places, up)
        for i in range(half):
            for k in range(momenta):
                row = (i * momenta + k) * size
                out[k, s, i] = part[k, s, start + i] + total[row : row + size]
    top = slab_of(info, slabs, 0)
    for k in range(momenta):
        to_first[k, 0] = out[k, top]
        to_second[k, 0] = out[k, slabs - 1 - top]


def halo_part(info, mixer, closer, field, part, halo, turn):
    momenta, slabs, energies, size, width = part.shape
    half = energies // 2
    edge = pltpu.VMEM((momenta, 1, half, size, width), jnp.float32)
    run = pltpu.VMEM((slabs, 2 * W - 1, momenta * size, width), jnp.bfloat16)
    return pl.pallas_call(
        functools.partial(halo_kernel, turn),
        out_shape=(pltpu.VMEM((momenta, slabs, half, size, width), jnp.float32), edge, edge),
        in_specs=[SMEM] + [VMEM] * 6,
        out_specs=(VMEM,) * 3,
        scratch_shapes=[run, run],
        compiler_params=PARAMS,
        name="halo_part",
    )(info, *near(mixer, closer, *field, part, halo))


def complex_matrix(block, sign):
    half = block.shape[-1] // 2
    swapped = jnp.concatenate([block[:, half:], block[:, :half]], axis=1)
    return jnp.concatenate([block, swapped * sign], axis=0)


def complex_product(left, right, sign):
    rows, width = left.shape
    lh, ll = split(left)
    rh, rl = split(complex_matrix(right, sign))
    y = dot(jnp.concatenate([lh, ll], axis=0), jnp.concatenate([rh, rl], axis=1))
    return y[:rows, :width] + y[:rows, width:] + y[rows:, :width]


def slab_of(info, slabs, turn):
    top = jnp.where(info[info.shape[0] - 1] == 1, 0, slabs - 1)
    return top if turn == 0 else slabs - 1 - top


def rimmed(info, summed, beside, k, turn, e):
    slabs = summed.shape[1]
    s = slab_of(info, slabs, turn)
    return s, summed[k, s, e] + neighbour_weight * (
        summed[k, slabs - 1 - s, e] + beside[turn][k, 0, e]
    )


def born_kernel(turn, info, green, summed, first, second, *refs):
    made, out, high_all, low_all = refs[-4:]
    momenta, slabs, energies, size, width = green.shape
    _, start = turn_of(info, energies, turn)
    lane = lax.broadcasted_iota(jnp.int32, (size, width), 1)
    sign = jnp.where(lane < width // 2, -1.0, 1.0).astype(jnp.float32)
    for k in range(momenta):
        for side in range(slabs):
            for i in range(energies // 2):
                s, field = rimmed(info, summed, (first, second), k, side, i)
                e = start + i
                g = green[k, s, e]
                new = g + complex_product(complex_product(g, field, sign), g, sign)
                made[k, s, i] = new
                out[k, s, e] = new
                high, low = split(new)
                high_all[s, e, k * size : (k + 1) * size] = high
                low_all[s, e, k * size : (k + 1) * size] = low


def born(info, green, summed, beside, turn, earlier=()):
    momenta, slabs, energies, size, width = green.shape
    return pl.pallas_call(
        functools.partial(born_kernel, turn),
        out_shape=(
            pltpu.VMEM((momenta, slabs, energies // 2, size, width), jnp.float32),
            pltpu.VMEM(green.shape, jnp.float32),
            *halves(*green.shape),
        ),
        in_specs=[SMEM] + [VMEM] * (4 + len(earlier)),
        out_specs=(VMEM,) * 4,
        input_output_aliases={5 + i: 1 + i for i in range(len(earlier))},
        compiler_params=PARAMS,
        name="born",
    )(info, *near(green, summed, *beside, *earlier))


def join_kernel(turn, info, summed, first, second, *refs):
    out, held, sems = refs[-3:]
    momenta, slabs, half = summed.shape[:3]
    _, start = turn_of(info, 2 * half, turn)
    copies = []
    for k in range(momenta):
        for side in range(slabs):
            for i in range(half):
                s, total = rimmed(info, summed, (first, second), k, side, i)
                held[k, s, i] = total
        copy = pltpu.make_async_copy(held.at[k], out.at[k, :, pl.ds(start, half)], sems.at[k])
        copy.start()
        copies.append(copy)
    for copy in copies:
        copy.wait()


def join(info, summed, beside, turn, earlier=()):
    momenta, slabs, half, size, width = summed.shape
    return pl.pallas_call(
        functools.partial(join_kernel, turn),
        out_shape=jax.ShapeDtypeStruct((momenta, slabs, 2 * half, size, width), jnp.float32),
        in_specs=[SMEM] + [VMEM] * 3 + [ANY] * len(earlier),
        out_specs=ANY,
        scratch_shapes=[
            pltpu.VMEM(summed.shape, jnp.float32),
            pltpu.SemaphoreType.DMA((momenta,)),
        ],
        input_output_aliases={4: 0} if earlier else {},
        compiler_params=PARAMS,
        name="join",
    )(info, *near(summed, *beside), *earlier)


ENERGY = ("energy", "mom")


def pairs(size, start):
    return [p for i in range(start, size - 1, 2) for p in ((i, i + 1), (i + 1, i))]


def swap_energy(x, turn):
    return lax.ppermute(x, ENERGY, pairs(lax.axis_size(ENERGY), turn))


def swap_slab(to_first, to_second):
    cores, size = lax.axis_size("energy"), lax.axis_size("slab")
    received = []
    for i, x in enumerate((to_first, to_second)):
        both = [
            (c * size + a, c * size + b)
            for c in range(cores)
            for a, b in pairs(size, (i + c) % 2)
        ]
        received.append(lax.ppermute(x, ("energy", "slab"), both))
    return received


TURNS = (0, 1)


def on_device(green, coupling, deformation, phonon_shifts):
    energies = green.shape[2]
    odd_energy = lax.axis_index(ENERGY) & 1
    odd_slab = (lax.axis_index("slab") + lax.axis_index("energy")) & 1
    info = jnp.concatenate([phonon_shifts, odd_energy[None], odd_slab[None]]).astype(jnp.int32)

    halo = []
    for turn in TURNS:
        start = jnp.where(odd_energy == turn, energies - W, 0)
        halo.append(swap_energy(lax.dynamic_slice_in_dim(green, start, W, axis=2), turn))
    mixer, closer, *field = prepare(coupling, deformation, green)

    def sums(field, halo):
        part = own_part(info, mixer, closer, field, green.shape)
        made = []
        for turn in TURNS:
            summed, a, b = halo_part(info, mixer, closer, field, part, halo[turn], turn)
            made.append((summed, swap_slab(a, b)))
        return made

    kept, first = (), sums(field, halo)
    halo = []
    for turn, (summed, beside) in enumerate(first):
        made, *kept = born(info, green, summed, beside, turn, kept)
        halo.append(swap_energy(made, turn))
    green_born, *field = kept

    result = ()
    for turn, (summed, beside) in enumerate(sums(field, halo)):
        result = (join(info, summed, beside, turn, result),)
    return green_born, *result


def solution(mesh):
    spread = P(None, "slab", ENERGY, None, None)
    return jax.shard_map(
        on_device,
        mesh=mesh,
        in_specs=(spread, P(), P(None, "slab", None, None), P()),
        out_specs=(spread, spread),
        check_vma=False,
    )
```

```python
import functools

import jax
import jax.numpy as jnp
from jax import lax
from jax.experimental import pallas as pl
from jax.experimental.pallas import tpu as pltpu
from jax.sharding import PartitionSpec as P

W = 2
neighbour_weight = 0.5

VMEM = pl.BlockSpec(memory_space=pltpu.VMEM)
ANY = pl.BlockSpec(memory_space=pl.ANY)
SMEM = pl.BlockSpec(memory_space=pltpu.SMEM)


PARAMS = pltpu.CompilerParams(vmem_limit_bytes=24 * 2**20)


def near(*arrays):
    return [pltpu.with_memory_space_constraint(x, pltpu.VMEM) for x in arrays]


def split(x):
    high = x.astype(jnp.bfloat16)
    low = (x - high.astype(jnp.float32)).astype(jnp.bfloat16)
    return high, low


def dot(a, b):
    return jnp.dot(a, b, preferred_element_type=jnp.float32)


def keep(high_all, low_all, s, place, blocks):
    high, low = split(jnp.concatenate(blocks, axis=0))
    high_all[s, place] = high
    low_all[s, place] = low


def prepare_kernel(coupling, deform, green, mixer, closer, high_all, low_all):
    modes, slabs, size, _ = deform.shape
    momenta = coupling.shape[1]
    for s in range(slabs):
        for e in range(green.shape[2]):
            keep(high_all, low_all, s, e, [green[k, s, e] for k in range(momenta)])
        for m in range(modes):
            d = deform[m, s]
            wide = jnp.concatenate([d] * momenta, axis=1)
            column = lax.broadcasted_iota(jnp.int32, wide.shape, 1) // size
            rows = []
            for k in range(momenta):
                weight = jnp.full(wide.shape, coupling[m, k, 0], jnp.float32)
                for k2 in range(1, momenta):
                    weight = jnp.where(column == k2, coupling[m, k, k2], weight)
                rows.append(weight * wide)
            high, low = split(jnp.concatenate(rows, axis=0))
            mixer[m, s] = jnp.concatenate([high, low], axis=1)
            flipped = d.T
            blank = jnp.zeros_like(flipped)
            both = jnp.concatenate(
                [
                    jnp.concatenate([flipped, blank], axis=1),
                    jnp.concatenate([blank, flipped], axis=1),
                ],
                axis=0,
            )
            high, low = split(both)
            closer[s, pl.ds(m * 2 * size, 2 * size), :] = jnp.concatenate([high, low], axis=1)


def halves(momenta, slabs, energies, size, width):
    return [pltpu.VMEM((slabs, energies, momenta * size, width), jnp.bfloat16)] * 2


def prepare(coupling, deformation, green):
    modes, slabs, size, _ = deformation.shape
    kron = coupling.shape[1] * size
    return pl.pallas_call(
        prepare_kernel,
        out_shape=(
            pltpu.VMEM((modes, slabs, kron, 2 * kron), jnp.bfloat16),
            pltpu.VMEM((slabs, modes * 2 * size, 4 * size), jnp.bfloat16),
            *halves(*green.shape),
        ),
        in_specs=[SMEM, VMEM, VMEM],
        out_specs=(VMEM,) * 4,
        compiler_params=PARAMS,
        name="prepare",
    )(coupling, *near(deformation, green))


def turn_of(info, energies, turn):
    up = info[info.shape[0] - 2] ^ (1 - turn)
    return up, up * (energies // 2)


def branch_sums(info, mixer, closer, high_all, low_all, s, places, up):
    modes, _, kron, _ = mixer.shape
    width = high_all.shape[3]
    highs, lows, ends = [], [], []
    for j in range(0, modes, 2):
        m = j + jnp.where((info[j] > 0) == (up == 1), 0, 1)
        at = [p + info[m] for p in places]
        gh = jnp.concatenate([high_all[s, a] for a in at], axis=1)
        gl = jnp.concatenate([low_all[s, a] for a in at], axis=1)
        mh = mixer[m, s, :, :kron]
        ml = mixer[m, s, :, kron:]
        left = dot(
            jnp.concatenate([mh, mh, ml], axis=1),
            jnp.concatenate([gh, gl, gh], axis=0),
        )
        high, low = split(left)
        count = len(places)
        highs.append(
            jnp.concatenate([high[:, i * width : (i + 1) * width] for i in range(count)], axis=0)
        )
        lows.append(
            jnp.concatenate([low[:, i * width : (i + 1) * width] for i in range(count)], axis=0)
        )
        ends.append(closer[s, pl.ds(pl.multiple_of(m * width, width), width), :])
    end = jnp.concatenate(ends, axis=0)
    both = dot(jnp.concatenate(highs, axis=1), end)
    rest = dot(jnp.concatenate(lows, axis=1), end[:, :width])
    return both[:, :width] + both[:, width:] + rest


def own_kernel(info, mixer, closer, high_all, low_all, out):
    momenta, slabs, energies, size, _ = out.shape
    half = energies // 2
    for s in range(slabs):
        for up in (1, 0):
            targets = range((1 - up) * half, (2 - up) * half)
            total = branch_sums(info, mixer, closer, high_all, low_all, s, targets, up)
            for i, e in enumerate(targets):
                for k in range(momenta):
                    row = (i * momenta + k) * size
                    out[k, s, e] = total[row : row + size]


def own_part(info, mixer, closer, field, shape):
    return pl.pallas_call(
        own_kernel,
        out_shape=pltpu.VMEM(shape, jnp.float32),
        in_specs=[SMEM] + [VMEM] * 4,
        out_specs=VMEM,
        compiler_params=PARAMS,
        name="own_part",
    )(info, *near(mixer, closer, *field))


def halo_kernel(turn, info, mixer, closer, high_own, low_own, part, halo, *refs):
    out, to_first, to_second, high_run, low_run = refs
    momenta, slabs, energies, size, _ = part.shape
    half = energies // 2
    up, start = turn_of(info, energies, turn)
    for s in range(slabs):
        for i in range(W - 1):
            own = jnp.where(up == 1, energies - W + 1 + i, i)
            place = jnp.where(up == 1, i, W + i)
            high_run[s, place] = high_own[s, own]
            low_run[s, place] = low_own[s, own]
        for i in range(W):
            place = jnp.where(up == 1, W - 1 + i, i)
            keep(high_run, low_run, s, place, [halo[k, s, i] for k in range(momenta)])
        shift = jnp.where(up == 1, -1, W)
        places = [i + shift for i in range(half)]
        total = branch_sums(info, mixer, closer, high_run, low_run, s, places, up)
        for i in range(half):
            for k in range(momenta):
                row = (i * momenta + k) * size
                out[k, s, i] = part[k, s, start + i] + total[row : row + size]
    top = slab_of(info, slabs, 0)
    for k in range(momenta):
        to_first[k, 0] = out[k, top]
        to_second[k, 0] = out[k, slabs - 1 - top]


def halo_part(info, mixer, closer, field, part, halo, turn):
    momenta, slabs, energies, size, width = part.shape
    half = energies // 2
    edge = pltpu.VMEM((momenta, 1, half, size, width), jnp.float32)
    run = pltpu.VMEM((slabs, 2 * W - 1, momenta * size, width), jnp.bfloat16)
    return pl.pallas_call(
        functools.partial(halo_kernel, turn),
        out_shape=(pltpu.VMEM((momenta, slabs, half, size, width), jnp.float32), edge, edge),
        in_specs=[SMEM] + [VMEM] * 6,
        out_specs=(VMEM,) * 3,
        scratch_shapes=[run, run],
        compiler_params=PARAMS,
        name="halo_part",
    )(info, *near(mixer, closer, *field, part, halo))


def complex_matrix(block, sign):
    half = block.shape[-1] // 2
    swapped = jnp.concatenate([block[:, half:], block[:, :half]], axis=1)
    return jnp.concatenate([block, swapped * sign], axis=0)


def complex_product(left, right, sign):
    rows, width = left.shape
    lh, ll = split(left)
    rh, rl = split(complex_matrix(right, sign))
    y = dot(jnp.concatenate([lh, ll], axis=0), jnp.concatenate([rh, rl], axis=1))
    return y[:rows, :width] + y[:rows, width:] + y[rows:, :width]


def slab_of(info, slabs, turn):
    top = jnp.where(info[info.shape[0] - 1] == 1, 0, slabs - 1)
    return top if turn == 0 else slabs - 1 - top


def rimmed(info, summed, beside, k, turn, e):
    slabs = summed.shape[1]
    s = slab_of(info, slabs, turn)
    return s, summed[k, s, e] + neighbour_weight * (
        summed[k, slabs - 1 - s, e] + beside[turn][k, 0, e]
    )


def born_kernel(turn, info, green, summed, first, second, *refs):
    made, out, high_all, low_all = refs[-4:]
    momenta, slabs, energies, size, width = green.shape
    _, start = turn_of(info, energies, turn)
    lane = lax.broadcasted_iota(jnp.int32, (size, width), 1)
    sign = jnp.where(lane < width // 2, -1.0, 1.0).astype(jnp.float32)
    for k in range(momenta):
        for side in range(slabs):
            for i in range(energies // 2):
                s, field = rimmed(info, summed, (first, second), k, side, i)
                e = start + i
                g = green[k, s, e]
                new = g + complex_product(complex_product(g, field, sign), g, sign)
                made[k, s, i] = new
                out[k, s, e] = new
                high, low = split(new)
                high_all[s, e, k * size : (k + 1) * size] = high
                low_all[s, e, k * size : (k + 1) * size] = low


def born(info, green, summed, beside, turn, earlier=()):
    momenta, slabs, energies, size, width = green.shape
    return pl.pallas_call(
        functools.partial(born_kernel, turn),
        out_shape=(
            pltpu.VMEM((momenta, slabs, energies // 2, size, width), jnp.float32),
            pltpu.VMEM(green.shape, jnp.float32),
            *halves(*green.shape),
        ),
        in_specs=[SMEM] + [VMEM] * (4 + len(earlier)),
        out_specs=(VMEM,) * 4,
        input_output_aliases={5 + i: 1 + i for i in range(len(earlier))},
        compiler_params=PARAMS,
        name="born",
    )(info, *near(green, summed, *beside, *earlier))


def join_kernel(turn, info, summed, first, second, *refs):
    out, held, sems = refs[-3:]
    momenta, slabs, half = summed.shape[:3]
    _, start = turn_of(info, 2 * half, turn)
    copies = []
    for k in range(momenta):
        for side in range(slabs):
            for i in range(half):
                s, total = rimmed(info, summed, (first, second), k, side, i)
                held[k, s, i] = total
        copy = pltpu.make_async_copy(held.at[k], out.at[k, :, pl.ds(start, half)], sems.at[k])
        copy.start()
        copies.append(copy)
    for copy in copies:
        copy.wait()


def join(info, summed, beside, turn, earlier=()):
    momenta, slabs, half, size, width = summed.shape
    return pl.pallas_call(
        functools.partial(join_kernel, turn),
        out_shape=jax.ShapeDtypeStruct((momenta, slabs, 2 * half, size, width), jnp.float32),
        in_specs=[SMEM] + [VMEM] * 3 + [ANY] * len(earlier),
        out_specs=ANY,
        scratch_shapes=[
            pltpu.VMEM(summed.shape, jnp.float32),
            pltpu.SemaphoreType.DMA((momenta,)),
        ],
        input_output_aliases={4: 0} if earlier else {},
        compiler_params=PARAMS,
        name="join",
    )(info, *near(summed, *beside), *earlier)


ENERGY = ("energy", "mom")


def pairs(size, start):
    return [p for i in range(start, size - 1, 2) for p in ((i, i + 1), (i + 1, i))]


def swap_energy(x, turn):
    return lax.ppermute(x, ENERGY, pairs(lax.axis_size(ENERGY), 1 - turn))


def swap_slab(to_first, to_second):
    cores, size = lax.axis_size("energy"), lax.axis_size("slab")
    received = []
    for i, x in enumerate((to_first, to_second)):
        both = [
            (c * size + a, c * size + b)
            for c in range(cores)
            for a, b in pairs(size, (i + c) % 2)
        ]
        received.append(lax.ppermute(x, ("energy", "slab"), both))
    return received


TURNS = (0, 1)


def on_device(green, coupling, deformation, phonon_shifts):
    energies = green.shape[2]
    low_first = (lax.axis_index(ENERGY) & 1) ^ 1
    below_first = (lax.axis_index("slab") + lax.axis_index("energy")) & 1
    info = jnp.concatenate([phonon_shifts, low_first[None], below_first[None]]).astype(jnp.int32)

    halo = []
    for turn in TURNS:
        start = jnp.where(low_first == turn, energies - W, 0)
        halo.append(swap_energy(lax.dynamic_slice_in_dim(green, start, W, axis=2), turn))
    mixer, closer, *field = prepare(coupling, deformation, green)

    def sums(field, halo):
        part = own_part(info, mixer, closer, field, green.shape)
        made = []
        for turn in TURNS:
            summed, a, b = halo_part(info, mixer, closer, field, part, halo[turn], turn)
            made.append((summed, swap_slab(a, b)))
        return made

    kept, first = (), sums(field, halo)
    halo = []
    for turn, (summed, beside) in enumerate(first):
        made, *kept = born(info, green, summed, beside, turn, kept)
        halo.append(swap_energy(made, turn))
    green_born, *field = kept

    result = ()
    for turn, (summed, beside) in enumerate(sums(field, halo)):
        result = (join(info, summed, beside, turn, result),)
    return green_born, *result


def solution(mesh):
    spread = P(None, "slab", ENERGY, None, None)
    return jax.shard_map(
        on_device,
        mesh=mesh,
        in_specs=(spread, P(), P(None, "slab", None, None), P()),
        out_specs=(spread, spread),
        check_vma=False,
    )
```

```python
import functools

import jax
import jax.numpy as jnp
from jax import lax
from jax.experimental import pallas as pl
from jax.experimental.pallas import tpu as pltpu
from jax.sharding import PartitionSpec as P

W = 2
neighbour_weight = 0.5

VMEM = pl.BlockSpec(memory_space=pltpu.VMEM)
ANY = pl.BlockSpec(memory_space=pl.ANY)
SMEM = pl.BlockSpec(memory_space=pltpu.SMEM)


PARAMS = pltpu.CompilerParams(vmem_limit_bytes=24 * 2**20)


def near(*arrays):
    return [pltpu.with_memory_space_constraint(x, pltpu.VMEM) for x in arrays]


def split(x):
    high = x.astype(jnp.bfloat16)
    low = (x - high.astype(jnp.float32)).astype(jnp.bfloat16)
    return high, low


def dot(a, b):
    return jnp.dot(a, b, preferred_element_type=jnp.float32)


def keep(high_all, low_all, s, place, blocks):
    high, low = split(jnp.concatenate(blocks, axis=0))
    high_all[s, place] = high
    low_all[s, place] = low


def prepare_kernel(coupling, deform, green, mixer, closer, high_all, low_all):
    modes, slabs, size, _ = deform.shape
    momenta = coupling.shape[1]
    for s in range(slabs):
        for e in range(green.shape[2]):
            keep(high_all, low_all, s, e, [green[k, s, e] for k in range(momenta)])
        for m in range(modes):
            d = deform[m, s]
            wide = jnp.concatenate([d] * momenta, axis=1)
            column = lax.broadcasted_iota(jnp.int32, wide.shape, 1) // size
            rows = []
            for k in range(momenta):
                weight = jnp.full(wide.shape, coupling[m, k, 0], jnp.float32)
                for k2 in range(1, momenta):
                    weight = jnp.where(column == k2, coupling[m, k, k2], weight)
                rows.append(weight * wide)
            high, low = split(jnp.concatenate(rows, axis=0))
            mixer[m, s] = jnp.concatenate([high, low], axis=1)
            flipped = d.T
            blank = jnp.zeros_like(flipped)
            both = jnp.concatenate(
                [
                    jnp.concatenate([flipped, blank], axis=1),
                    jnp.concatenate([blank, flipped], axis=1),
                ],
                axis=0,
            )
            high, low = split(both)
            closer[s, pl.ds(m * 2 * size, 2 * size), :] = jnp.concatenate([high, low], axis=1)


def halves(momenta, slabs, energies, size, width):
    return [pltpu.VMEM((slabs, energies, momenta * size, width), jnp.bfloat16)] * 2


def prepare(coupling, deformation, green):
    modes, slabs, size, _ = deformation.shape
    kron = coupling.shape[1] * size
    return pl.pallas_call(
        prepare_kernel,
        out_shape=(
            pltpu.VMEM((modes, slabs, kron, 2 * kron), jnp.bfloat16),
            pltpu.VMEM((slabs, modes * 2 * size, 4 * size), jnp.bfloat16),
            *halves(*green.shape),
        ),
        in_specs=[SMEM, VMEM, VMEM],
        out_specs=(VMEM,) * 4,
        compiler_params=PARAMS,
        name="prepare",
    )(coupling, *near(deformation, green))


def turn_of(info, energies, turn):
    up = info[info.shape[0] - 2] ^ (1 - turn)
    return up, up * (energies // 2)


def branch_sums(info, mixer, closer, high_all, low_all, s, places, up):
    modes, _, kron, _ = mixer.shape
    width = high_all.shape[3]
    highs, lows, ends = [], [], []
    for j in range(0, modes, 2):
        m = j + jnp.where((info[j] > 0) == (up == 1), 0, 1)
        at = [p + info[m] for p in places]
        gh = jnp.concatenate([high_all[s, a] for a in at], axis=1)
        gl = jnp.concatenate([low_all[s, a] for a in at], axis=1)
        mh = mixer[m, s, :, :kron]
        ml = mixer[m, s, :, kron:]
        left = dot(
            jnp.concatenate([mh, mh, ml], axis=1),
            jnp.concatenate([gh, gl, gh], axis=0),
        )
        high, low = split(left)
        count = len(places)
        highs.append(
            jnp.concatenate([high[:, i * width : (i + 1) * width] for i in range(count)], axis=0)
        )
        lows.append(
            jnp.concatenate([low[:, i * width : (i + 1) * width] for i in range(count)], axis=0)
        )
        ends.append(closer[s, pl.ds(pl.multiple_of(m * width, width), width), :])
    end = jnp.concatenate(ends, axis=0)
    both = dot(jnp.concatenate(highs, axis=1), end)
    rest = dot(jnp.concatenate(lows, axis=1), end[:, :width])
    return both[:, :width] + both[:, width:] + rest


def own_kernel(info, mixer, closer, high_all, low_all, out):
    momenta, slabs, energies, size, _ = out.shape
    half = energies // 2
    for s in range(slabs):
        for up in (1, 0):
            targets = range((1 - up) * half, (2 - up) * half)
            total = branch_sums(info, mixer, closer, high_all, low_all, s, targets, up)
            for i, e in enumerate(targets):
                for k in range(momenta):
                    row = (i * momenta + k) * size
                    out[k, s, e] = total[row : row + size]


def own_part(info, mixer, closer, field, shape):
    return pl.pallas_call(
        own_kernel,
        out_shape=pltpu.VMEM(shape, jnp.float32),
        in_specs=[SMEM] + [VMEM] * 4,
        out_specs=VMEM,
        compiler_params=PARAMS,
        name="own_part",
    )(info, *near(mixer, closer, *field))


def halo_kernel(turn, info, mixer, closer, high_own, low_own, part, halo, *refs):
    out, to_first, to_second, high_run, low_run = refs
    momenta, slabs, energies, size, _ = part.shape
    half = energies // 2
    up, start = turn_of(info, energies, turn)
    for s in range(slabs):
        for i in range(W - 1):
            own = jnp.where(up == 1, energies - W + 1 + i, i)
            place = jnp.where(up == 1, i, W + i)
            high_run[s, place] = high_own[s, own]
            low_run[s, place] = low_own[s, own]
        for i in range(W):
            place = jnp.where(up == 1, W - 1 + i, i)
            keep(high_run, low_run, s, place, [halo[k, s, i] for k in range(momenta)])
        shift = jnp.where(up == 1, -1, W)
        places = [i + shift for i in range(half)]
        total = branch_sums(info, mixer, closer, high_run, low_run, s, places, up)
        for i in range(half):
            for k in range(momenta):
                row = (i * momenta + k) * size
                out[k, s, i] = part[k, s, start + i] + total[row : row + size]
    top = slab_of(info, slabs, 0)
    for k in range(momenta):
        to_first[k, 0] = out[k, top]
        to_second[k, 0] = out[k, slabs - 1 - top]


def halo_part(info, mixer, closer, field, part, halo, turn):
    momenta, slabs, energies, size, width = part.shape
    half = energies // 2
    edge = pltpu.VMEM((momenta, 1, half, size, width), jnp.float32)
    run = pltpu.VMEM((slabs, 2 * W - 1, momenta * size, width), jnp.bfloat16)
    return pl.pallas_call(
        functools.partial(halo_kernel, turn),
        out_shape=(pltpu.VMEM((momenta, slabs, half, size, width), jnp.float32), edge, edge),
        in_specs=[SMEM] + [VMEM] * 6,
        out_specs=(VMEM,) * 3,
        scratch_shapes=[run, run],
        compiler_params=PARAMS,
        name="halo_part",
    )(info, *near(mixer, closer, *field, part, halo))


def complex_matrix(block, sign):
    half = block.shape[-1] // 2
    swapped = jnp.concatenate([block[:, half:], block[:, :half]], axis=1)
    return jnp.concatenate([block, swapped * sign], axis=0)


def complex_product(left, right, sign):
    rows, width = left.shape
    lh, ll = split(left)
    rh, rl = split(complex_matrix(right, sign))
    y = dot(jnp.concatenate([lh, ll], axis=0), jnp.concatenate([rh, rl], axis=1))
    return y[:rows, :width] + y[:rows, width:] + y[rows:, :width]


def slab_of(info, slabs, turn):
    top = jnp.where(info[info.shape[0] - 1] == 1, 0, slabs - 1)
    return top if turn == 0 else slabs - 1 - top


def rimmed(info, summed, beside, k, turn, e):
    slabs = summed.shape[1]
    s = slab_of(info, slabs, turn)
    return s, summed[k, s, e] + neighbour_weight * (
        summed[k, slabs - 1 - s, e] + beside[turn][k, 0, e]
    )


def born_kernel(turn, info, green, summed, first, second, *refs):
    made, out, high_all, low_all = refs[-4:]
    momenta, slabs, energies, size, width = green.shape
    _, start = turn_of(info, energies, turn)
    lane = lax.broadcasted_iota(jnp.int32, (size, width), 1)
    sign = jnp.where(lane < width // 2, -1.0, 1.0).astype(jnp.float32)
    for k in range(momenta):
        for side in range(slabs):
            for i in range(energies // 2):
                s, field = rimmed(info, summed, (first, second), k, side, i)
                e = start + i
                g = green[k, s, e]
                new = g + complex_product(complex_product(g, field, sign), g, sign)
                made[k, s, i] = new
                out[k, s, e] = new
                high, low = split(new)
                high_all[s, e, k * size : (k + 1) * size] = high
                low_all[s, e, k * size : (k + 1) * size] = low


def born(info, green, summed, beside, turn, earlier=()):
    momenta, slabs, energies, size, width = green.shape
    return pl.pallas_call(
        functools.partial(born_kernel, turn),
        out_shape=(
            pltpu.VMEM((momenta, slabs, energies // 2, size, width), jnp.float32),
            pltpu.VMEM(green.shape, jnp.float32),
            *halves(*green.shape),
        ),
        in_specs=[SMEM] + [VMEM] * (4 + len(earlier)),
        out_specs=(VMEM,) * 4,
        input_output_aliases={5 + i: 1 + i for i in range(len(earlier))},
        compiler_params=PARAMS,
        name="born",
    )(info, *near(green, summed, *beside, *earlier))


def join_kernel(turn, info, summed, first, second, *refs):
    out, held, sems = refs[-3:]
    momenta, slabs, half = summed.shape[:3]
    _, start = turn_of(info, 2 * half, turn)
    copies = []
    for k in range(momenta):
        for side in range(slabs):
            for i in range(half):
                s, total = rimmed(info, summed, (first, second), k, side, i)
                held[k, s, i] = total
        copy = pltpu.make_async_copy(held.at[k], out.at[k, :, pl.ds(start, half)], sems.at[k])
        copy.start()
        copies.append(copy)
    for copy in copies:
        copy.wait()


def join(info, summed, beside, turn, earlier=()):
    momenta, slabs, half, size, width = summed.shape
    return pl.pallas_call(
        functools.partial(join_kernel, turn),
        out_shape=jax.ShapeDtypeStruct((momenta, slabs, 2 * half, size, width), jnp.float32),
        in_specs=[SMEM] + [VMEM] * 3 + [ANY] * len(earlier),
        out_specs=ANY,
        scratch_shapes=[
            pltpu.VMEM(summed.shape, jnp.float32),
            pltpu.SemaphoreType.DMA((momenta,)),
        ],
        input_output_aliases={4: 0} if earlier else {},
        compiler_params=PARAMS,
        name="join",
    )(info, *near(summed, *beside), *earlier)


ENERGY = ("energy", "mom")


def pairs(size, start):
    return [p for i in range(start, size - 1, 2) for p in ((i, i + 1), (i + 1, i))]


def swap_energy(x, turn):
    return lax.ppermute(x, ENERGY, pairs(lax.axis_size(ENERGY), 1 - turn))


def swap_slab(to_first, to_second):
    cores, size = lax.axis_size("energy"), lax.axis_size("slab")
    received = []
    for i, x in enumerate((to_first, to_second)):
        both = [
            (c * size + a, c * size + b)
            for c in range(cores)
            for a, b in pairs(size, i)
        ]
        received.append(lax.ppermute(x, ("energy", "slab"), both))
    return received


TURNS = (0, 1)


def on_device(green, coupling, deformation, phonon_shifts):
    energies = green.shape[2]
    low_first = (lax.axis_index(ENERGY) & 1) ^ 1
    below_first = lax.axis_index("slab") & 1
    info = jnp.concatenate([phonon_shifts, low_first[None], below_first[None]]).astype(jnp.int32)

    halo = []
    for turn in TURNS:
        start = jnp.where(low_first == turn, energies - W, 0)
        halo.append(swap_energy(lax.dynamic_slice_in_dim(green, start, W, axis=2), turn))
    mixer, closer, *field = prepare(coupling, deformation, green)

    def sums(field, halo):
        part = own_part(info, mixer, closer, field, green.shape)
        made = []
        for turn in TURNS:
            summed, a, b = halo_part(info, mixer, closer, field, part, halo[turn], turn)
            made.append((summed, swap_slab(a, b)))
        return made

    kept, first = (), sums(field, halo)
    halo = []
    for turn, (summed, beside) in enumerate(first):
        made, *kept = born(info, green, summed, beside, turn, kept)
        halo.append(swap_energy(made, turn))
    green_born, *field = kept

    result = ()
    for turn, (summed, beside) in enumerate(sums(field, halo)):
        result = (join(info, summed, beside, turn, result),)
    return green_born, *result


def solution(mesh):
    spread = P(None, "slab", ENERGY, None, None)
    return jax.shard_map(
        on_device,
        mesh=mesh,
        in_specs=(spread, P(), P(None, "slab", None, None), P()),
        out_specs=(spread, spread),
        check_vma=False,
    )
```
